256 devices in a mesh: tp: 8 (over y, core), ep: 32 (over z, x).
Axes of the slice: x: 4, y: 4, z: 8, core: 2. Of those that a mesh axis runs over, the one named last changes fastest.
Arguments:
- tokens: bfloat16 [512, 8192], P('ep'), may hold values from -6 to 6
- cotangent: bfloat16 [512, 8192], P('ep'), may hold values from -6 to 6
- w_gate: bfloat16 [14336, 8192], P(('tp', 'ep')), may hold values from -0.0625 to 0.0625
- w_up: bfloat16 [14336, 8192], P(('tp', 'ep')), may hold values from -0.0625 to 0.0625
- w_down: bfloat16 [14336, 8192], P(('tp', 'ep')), may hold values from -0.375 to 0.375
- neuron_expert: int32 [14336], P(('tp', 'ep')), may hold values from 0 to 63, as said below
- neuron_slot: int32 [14336], P(('tp', 'ep')), may hold values from 0 to 63, as said below
- choice_expert: int32 [512, 8], P('ep'), may hold values from 0 to 63, all different within a row; in each aligned block of 16 rows (0 to 15, 16 to 31, ...) at most 4 rows name the same one
- choice_weight: float32 [512, 8], P('ep'), may hold values from 0.02 to 0.3
Outputs:
- output: bfloat16 [512, 8192], P('ep', 'tp')
- d_tokens: bfloat16 [512, 8192], P('ep', 'tp')
- d_weight: float32 [512, 8], P('ep')
- d_gate_exp: bfloat16 [64, 512, 8192], P('ep', 'tp')
- d_up_exp: bfloat16 [64, 512, 8192], P('ep', 'tp')
- d_down_exp: bfloat16 [64, 512, 8192], P('ep', 'tp')
The draws below stay inside these ranges and needn't reach their ends.
Inputs may be any that keep to these rules, and one draw needn't show every extreme that they name: `neuron_expert`: expert e belongs to ep index e // 2. Among the 56 neurons starting at any multiple of 56, at most 4 name experts of one ep index. `neuron_slot`: within each tp range of 1792 neurons, the neurons of one expert have distinct slots. `choice_expert`: each row names 8 different experts; in each aligned block of 16 rows no expert is named more than 4 times.
All inputs are finite; a program needn't handle non-finite values.
Results may differ from the reference program's by a relative error of at most 0.018.
Values may be sent and summed in bfloat16 or wider, within the bound.
No kernel may reach another device: no remote copies, remote signals or barrier semaphores. Data moves between devices by JAX's collectives and lax.ppermute only.
A program may use at most 128 MiB of HBM per device.

```python
import math
import jax
import jax.numpy as jnp
import numpy as np
from jax import lax

D = 8192
NL = 56
E_DEV = 2
TOPK = 8
TOK_DEV = 16
FF = 14336
EXPERTS = 64
PEER = 4
CAPN = 64
HID = 512
TCAP = 4
TOKENS = 512
N_TP = 8
N_EP = 32


def neuron_tables(key):
    base = jax.random.fold_in(key, 7)

    def one_group(group_key):
        key_hot, key_source, key_flip = jax.random.split(group_key, 3)
        hot = jax.random.randint(key_hot, (), 0, N_EP)
        others = (hot + 1 + jnp.repeat(jnp.arange(N_EP - 1, dtype=jnp.int32), PEER)) % N_EP

        def one_source(source_key):
            key_pick, key_order = jax.random.split(source_key)
            picked = jax.random.permutation(key_pick, others)[:NL - PEER]
            owners = jnp.concatenate([jnp.full((PEER,), hot, jnp.int32), picked.astype(jnp.int32)])
            return jax.random.permutation(key_order, owners)
        owners = jax.vmap(one_source)(jax.random.split(key_source, N_EP)).reshape(-1)
        onehot = (owners[:, None] == jnp.arange(N_EP, dtype=jnp.int32)[None, :]).astype(jnp.int32)
        before = jnp.cumsum(onehot, 0) - onehot
        rank = jnp.sum(before * onehot, 1)
        flip = jax.random.randint(key_flip, (N_EP,), 0, E_DEV)
        local = (rank + flip[owners]) % E_DEV
        return (owners * E_DEV + local, rank // E_DEV)
    experts, slots = jax.vmap(one_group)(jax.random.split(base, N_TP))
    return (experts.reshape(-1).astype(jnp.int32), slots.reshape(-1).astype(jnp.int32))


def draw_neuron_expert(key, part):
    return neuron_tables(key)[0]


def draw_neuron_slot(key, part):
    return neuron_tables(key)[1]


def levels(stream_key, shape, shards, low, largest):
    gain, own = 1.0, jax.random.fold_in(stream_key, 6)
    for dim, blocks in shards:
        heights = jnp.exp(jax.random.uniform(jax.random.fold_in(own, dim), (blocks,), jnp.float32, low / len(shards), largest / len(shards)))
        gain = gain * jnp.repeat(heights, shape[dim] // blocks).reshape([-1 if axis == dim else 1 for axis in range(len(shape))])
    return gain


def deal_out(rng, own, number, rows, amount, top, most, slope):
    sequence = jax.random.permutation(rng, amount)
    packed, ordinary = load_shares(amount, rows * top, most, slope, True), load_shares(amount, rows * top, most, slope, False)
    places = jnp.arange(amount)

    def named(lengths, turn):
        used = int((lengths > 0).sum())
        fixed = max(1, used // 4)
        passed = fixed + (places - fixed + turn * (used - fixed)) % max(1, amount - fixed)
        return jnp.zeros((amount,), jnp.int32).at[sequence[jnp.where(places < fixed, places, passed)]].set(jnp.asarray(lengths, jnp.int32))

    lengths = jnp.where(number % 4 == 0, named(packed, number // 4), named(ordinary, number - number // 4 - 1))
    mixed = jax.random.permutation(jax.random.fold_in(own, 3), amount)
    source_of, receiver = mixed[0:amount // 2 * 2:2], mixed[1:amount // 2 * 2:2]
    room = jnp.minimum(lengths[source_of] - 1, most - lengths[receiver]) // 2
    room = jnp.where((source_of == sequence[0]) | (receiver == sequence[0]) | (lengths[receiver] == 0), 0, jnp.maximum(room, 0))
    passed = jax.random.randint(jax.random.fold_in(own, 4), (amount // 2,), 0, 1 << 20) % (room + 1)
    lengths = lengths.at[source_of].add(-passed).at[receiver].add(passed)
    members = jnp.searchsorted(jnp.cumsum(lengths), jnp.arange(rows * top), side="right").astype(jnp.int32)
    grid = members.reshape(top, rows).T
    grid = grid[jax.random.permutation(jax.random.fold_in(own, 1), rows)]
    turn = jax.random.randint(jax.random.fold_in(own, 2), (rows, 1), 0, top)
    return jnp.take_along_axis(grid, (jnp.arange(top)[None, :] + turn) % top, axis=1)


def load_shares(count, total, limit, slope, full):
    weights = [(1 << 20) // math.isqrt(standing ** slope) + 1 for standing in range(1, count + 1)]
    largest = limit if full else min(limit, max(-(-total // count), total * weights[0] // sum(weights)))
    least = 1 if total - largest >= count - 1 else 0
    given, rest = [largest] + [least] * (count - 1), total - largest - least * (count - 1)
    while rest > 0:
        movable = [i for i in range(1, count) if given[i] < largest] or [i for i in range(1, count) if given[i] < limit]
        mass, budget = sum([weights[i] for i in movable]), rest
        for i in movable:
            more = min(limit - given[i], max(1, budget * weights[i] // mass), rest)
            given[i] = given[i] + more
            rest = rest - more
    return np.array(given)


def normal_values(rng, dims, width, bound, cuts=(), held_as=jnp.bfloat16):
    level = levels(rng, dims, cuts, -0.22, 0.18) if cuts else 1.0
    entries = jax.random.normal(rng, dims, jnp.float32) * width * level
    return jnp.minimum(jnp.maximum(entries, -bound), bound).astype(held_as)


def setup_inputs(seed: int = 0) -> dict:
    seeds = jax.random.split(jax.random.key(seed), 10)
    tokens = normal_values(seeds[0], (TOKENS, D), 1.0, 6.0, ((0, 32),))
    cotangent = normal_values(seeds[1], (TOKENS, D), 1.0, 6.0, ((0, 32),))
    w_gate = normal_values(seeds[2], (FF, D), D ** -0.5, 0.0625, ((0, 256),))
    w_up = normal_values(seeds[3], (FF, D), D ** -0.5, 0.0625, ((0, 256),))
    w_down = normal_values(seeds[4], (FF, D), (NL * N_TP // E_DEV) ** -0.5, 0.375, ((0, 256),))
    neuron_expert = draw_neuron_expert(jax.random.fold_in(seeds[9], 71), 0)
    neuron_slot = draw_neuron_slot(jax.random.fold_in(seeds[9], 71), 0)
    choice_expert_keys = jax.random.split(jax.random.fold_in(seeds[7], 1), TOKENS // TOK_DEV)
    choice_expert_turns = jax.random.permutation(jax.random.fold_in(seeds[7], 3), TOKENS // TOK_DEV)
    choice_expert = jax.vmap(lambda own, number: deal_out(jax.random.fold_in(seeds[7], 2), own, number, TOK_DEV, EXPERTS, TOPK, TCAP, 1))(choice_expert_keys, choice_expert_turns).reshape((TOKENS, TOPK))
    choice_weight = jnp.clip(0.02 + 0.28 * jax.random.uniform(seeds[8], (TOKENS, TOPK), jnp.float32) ** levels(seeds[8], (TOKENS, TOPK), ((0, 32),), -0.2, 0.2), 0.02, 0.3)
    return {"tokens": tokens, "cotangent": cotangent, "w_gate": w_gate, "w_up": w_up, "w_down": w_down, "neuron_expert": neuron_expert, "neuron_slot": neuron_slot, "choice_expert": choice_expert, "choice_weight": choice_weight}


def slope_of(gate):
    sig = jax.nn.sigmoid(gate)
    return sig * (1.0 + gate * (1.0 - sig))


def block_sums(pairs):
    total = None
    for left, right in pairs:
        parts = jnp.einsum('rtc,tcd->rtd', left.reshape(-1, N_TP, CAPN).astype(jnp.float32), right.reshape(N_TP, CAPN, D).astype(jnp.float32))
        total = parts if total is None else total + parts
    rounded = lax.optimization_barrier(total.astype(jnp.bfloat16))
    return jnp.sum(rounded.astype(jnp.float32), 1)


def reference(tokens, cotangent, w_gate, w_up, w_down, neuron_expert, neuron_slot, choice_expert, choice_weight):
    neuron = jnp.arange(FF, dtype=jnp.int32)
    dest = (neuron_expert * HID + (neuron // (FF // N_TP)) * CAPN + neuron_slot).astype(jnp.int32)

    def layout(weight):
        return jnp.zeros((EXPERTS * HID, D), jnp.bfloat16).at[dest].set(weight).reshape(EXPERTS, HID, D)

    gate_exp = layout(w_gate)
    up_exp = layout(w_up)
    down_exp = layout(w_down)
    count = TOK_DEV * TOPK
    flat = choice_expert.reshape(N_EP, count)
    row_iota = lax.broadcasted_iota(jnp.int32, (count, count), 0)
    col_iota = lax.broadcasted_iota(jnp.int32, (count, count), 1)
    same = (flat[:, :, None] == flat[:, None, :]) & (col_iota < row_iota)[None]
    rank = jnp.sum(same.astype(jnp.int32), 2)
    source = jnp.arange(N_EP, dtype=jnp.int32)[:, None]
    slot_index = ((flat * N_EP + source) * TCAP + rank).reshape(-1).astype(jnp.int32)
    token_index = (jnp.arange(TOKENS * TOPK, dtype=jnp.int32) // TOPK).astype(jnp.int32)
    rows_expert = N_EP * TCAP
    x_disp = jnp.zeros((EXPERTS * rows_expert, D), jnp.bfloat16).at[slot_index].set(tokens[token_index]).reshape(EXPERTS, rows_expert, D)

    def forward(items):
        x_rows, w_g, w_u, w_d = items
        gate = jnp.dot(x_rows, w_g.T, preferred_element_type=jnp.float32)
        upper = jnp.dot(x_rows, w_u.T, preferred_element_type=jnp.float32)
        hidden = (jax.nn.silu(gate) * upper).astype(jnp.bfloat16)
        result = block_sums([(hidden, w_d)]).astype(jnp.bfloat16)
        return result, gate, upper

    outs, gates, uppers = lax.map(forward, (x_disp, gate_exp, up_exp, down_exp))
    per_choice = outs.reshape(-1, D)[slot_index].astype(jnp.float32).reshape(TOKENS, TOPK, D)
    output = jnp.sum(choice_weight[:, :, None] * per_choice, 1).astype(jnp.bfloat16)
    d_weight = jnp.sum(per_choice * cotangent.astype(jnp.float32)[:, None, :], 2)
    scaled = (choice_weight[:, :, None] * cotangent.astype(jnp.float32)[:, None, :]).astype(jnp.bfloat16).reshape(-1, D)
    g_disp = jnp.zeros((EXPERTS * rows_expert, D), jnp.bfloat16).at[slot_index].set(scaled).reshape(EXPERTS, rows_expert, D)

    def backward(items):
        x_rows, g_rows, gate, upper, w_g, w_u, w_d = items
        hidden = (jax.nn.silu(gate) * upper).astype(jnp.bfloat16)
        d_hidden = jnp.dot(g_rows, w_d.T, preferred_element_type=jnp.float32)
        d_down = jnp.dot(hidden.T, g_rows, preferred_element_type=jnp.float32).astype(jnp.bfloat16)
        d_gate_rows = (d_hidden * upper * slope_of(gate)).astype(jnp.bfloat16)
        d_up_rows = (d_hidden * jax.nn.silu(gate)).astype(jnp.bfloat16)
        d_gate = jnp.dot(d_gate_rows.T, x_rows, preferred_element_type=jnp.float32).astype(jnp.bfloat16)
        d_up = jnp.dot(d_up_rows.T, x_rows, preferred_element_type=jnp.float32).astype(jnp.bfloat16)
        d_rows = block_sums([(d_gate_rows, w_g), (d_up_rows, w_u)]).astype(jnp.bfloat16)
        return d_rows, d_gate, d_up, d_down

    d_rows, d_gate_exp, d_up_exp, d_down_exp = lax.map(backward, (x_disp, g_disp, gates, uppers, gate_exp, up_exp, down_exp))
    d_choice = d_rows.reshape(-1, D)[slot_index].astype(jnp.float32).reshape(TOKENS, TOPK, D)
    d_tokens = jnp.sum(d_choice, 1).astype(jnp.bfloat16)
    return output, d_tokens, d_weight, d_gate_exp, d_up_exp, d_down_exp
```

```python
import jax
import jax.numpy as jnp
from jax import lax
from jax.sharding import PartitionSpec as P

NX = 4
NZ = 8
NY = 4
PEER = 4
CAPN = 64
EXPERTS = 64
E_DEV = 2
TCAP = 128
BF = jnp.bfloat16
F32 = jnp.float32


def move_x(v, s):
    pairs = [(z * NX + x, z * NX + (x + s) % NX) for z in range(NZ) for x in range(NX)]
    return lax.ppermute(v, "ep", pairs)


def move_z(v, s):
    pairs = [(z * NX + x, (z + s) % NZ * NX + x) for z in range(NZ) for x in range(NX)]
    return lax.ppermute(v, "ep", pairs)


def move_y(v, s):
    pairs = [(y * 2 + c, (y + s) % NY * 2 + c) for y in range(NY) for c in range(2)]
    return lax.ppermute(v, "tp", pairs)


def swap_core(v):
    return lax.ppermute(v, "tp", [(i, i ^ 1) for i in range(2 * NY)])


def mm(a, b, dims):
    return lax.dot_general(a, b, (dims, ((), ())), preferred_element_type=F32)


def gather_tokens(block):
    base = jnp.stack([block, move_x(block, -1), move_x(block, -2), move_x(block, 1)], 0)
    up = [base]
    down = []
    for _ in range(3):
        up.append(move_z(up[-1], -1))
        down.append(move_z(down[-1] if down else base, 1))
    far = jnp.concatenate([move_z(up[3][:2], -1), move_z(down[2][2:], 1)], 0)
    return jnp.stack(up + [far] + down[::-1], 1)


def exchange_weights(w_gate, w_up, w_down, y, c):
    width = w_gate.shape[1]
    two = width // NY
    one = two // 2

    def piece(s):
        start = (y + s) % NY * two
        rows = [lax.dynamic_slice_in_dim(w, start, two, 1) for w in (w_gate, w_up, w_down)]
        return jnp.concatenate(rows, 0)

    got = [piece(0)] + [move_y(piece(-s % NY), -s) for s in range(1, NY)]
    mine = [lax.dynamic_slice_in_dim(g, c * one, one, 1) for g in got]
    other = [lax.dynamic_slice_in_dim(g, (1 - c) * one, one, 1) for g in got]
    swapped = swap_core(jnp.stack(other, 0))
    return jnp.stack([jnp.stack(mine, 0), swapped], 1)


def gather_tp(v):
    near = jnp.stack([v] + [move_y(v, -s) for s in range(1, NY)], 0)
    return jnp.stack([near, swap_core(near)], 1)


def reduce_tp(parts):
    half = parts[:, 0] + swap_core(parts[:, 1].astype(BF)).astype(F32)
    total = half[0]
    for s in range(1, NY):
        total = total + move_y(half[s].astype(BF), s).astype(F32)
    return total


def reduce_ep(parts):
    total = parts[0].astype(F32)
    for s in range(1, NX):
        total = total + move_x(parts[s], s).astype(F32)
    half = total.astype(BF)
    out = total[0]
    for s in range(1, NZ):
        out = out + move_z(half[s], s).astype(F32)
    return out


def body(
    tokens,
    cotangent,
    w_gate,
    w_up,
    w_down,
    neuron_expert,
    neuron_slot,
    choice_expert,
    choice_weight,
):
    t = lax.axis_index("tp")
    ep = lax.axis_index("ep")
    y, c = t // 2, t % 2
    z, x = ep // NX, ep % NX
    n_ep = NX * NZ
    nl, width = w_gate.shape
    tok = tokens.shape[0]
    lw = width // (2 * NY)
    n_tok = n_ep * tok

    experts = lax.broadcasted_iota(jnp.int32, (tok, choice_expert.shape[1], EXPERTS), 2)
    picked = choice_expert[:, :, None] == experts
    dense_w = jnp.sum(jnp.where(picked, choice_weight[:, :, None], 0.0), 1)
    w_hi = dense_w.astype(BF)
    w_lo = (dense_w - w_hi.astype(F32)).astype(BF)
    block = jnp.concatenate(
        [
            lax.dynamic_slice_in_dim(tokens, t * lw, lw, 1),
            lax.dynamic_slice_in_dim(cotangent, t * lw, lw, 1),
            w_hi,
            w_lo,
        ],
        1,
    )
    rows = gather_tokens(block).reshape(n_tok, 2 * lw + 2 * EXPERTS)
    xs = rows[:, :lw]
    cs = rows[:, lw : 2 * lw]
    hi = rows[:, 2 * lw : 2 * lw + EXPERTS]
    lo = rows[:, 2 * lw + EXPERTS :]

    weights = exchange_weights(w_gate, w_up, w_down, y, c)
    w_gu = weights[:, :, : 2 * nl].reshape(-1, lw)
    w_d = weights[:, :, 2 * nl :].reshape(-1, lw)

    part_gu = mm(w_gu, xs, ((1,), (1,))).reshape(NY, 2, 2 * nl, n_tok)
    part_d = mm(w_d, cs, ((1,), (1,))).reshape(NY, 2, nl, n_tok)
    sums = reduce_tp(jnp.concatenate([part_gu, part_d], 2))
    gate, upper, d_raw = sums[:nl], sums[nl : 2 * nl], sums[2 * nl :]

    onehot = (
        neuron_expert[:, None] == lax.broadcasted_iota(jnp.int32, (nl, EXPERTS), 1)
    ).astype(BF)
    scale = mm(onehot, hi, ((1,), (1,))) + mm(onehot, lo, ((1,), (1,)))
    sig = jax.nn.sigmoid(gate)
    silu = gate * sig
    hidden = silu * upper
    dh = d_raw * scale
    coefs = jnp.concatenate(
        [dh * upper * sig * (1.0 + gate * (1.0 - sig)), dh * silu, hidden * scale], 0
    ).astype(BF)
    q_exp = mm(onehot, (hidden * d_raw).astype(BF), ((0,), (0,))).astype(BF)

    everyone = gather_tp(jnp.concatenate([coefs, q_exp], 0))
    c_gu = everyone[:, :, : 2 * nl].reshape(-1, n_tok)
    c_h = everyone[:, :, 2 * nl : 3 * nl].reshape(-1, n_tok)
    q_all = jnp.sum(everyone[:, :, 3 * nl :].astype(F32), (0, 1))
    out_part = mm(c_h, w_d, ((0,), (0,))).astype(BF)
    dx_part = mm(c_gu, w_gu, ((0,), (0,))).astype(BF)
    q_part = jnp.pad(q_all.T.astype(BF), ((0, 0), (0, EXPERTS)))
    parts = jnp.concatenate([out_part, dx_part, q_part], 1)
    final = reduce_ep(parts.reshape(NX, NZ, tok, -1))
    output = final[:, :lw].astype(BF)
    d_tokens = final[:, lw : 2 * lw].astype(BF)
    q_mine = final[:, 2 * lw : 2 * lw + EXPERTS]
    d_weight = jnp.sum(jnp.where(picked, q_mine[:, None, :], 0.0), 2)

    ri = lax.broadcasted_iota(jnp.int32, (n_tok, n_tok), 0)
    ci = lax.broadcasted_iota(jnp.int32, (n_tok, n_tok), 1)
    per_x = n_tok // NX
    place = (ri // per_x + x) % NX * per_x + (ri // tok % NZ + z) % NZ * tok + ri % tok
    to_common = (place == ci).astype(BF)
    earlier = (ci <= ri).astype(BF)
    own = lax.broadcasted_iota(jnp.int32, (EXPERTS, E_DEV), 0) == (
        ep * E_DEV + lax.broadcasted_iota(jnp.int32, (EXPERTS, E_DEV), 1)
    )
    chosen = (mm(hi, own.astype(BF), ((1,), (0,))) > 0.0).astype(BF)
    rank = mm(earlier, chosen, ((1,), (0,))).astype(jnp.int32) - 1
    slots = lax.broadcasted_iota(jnp.int32, (n_tok, TCAP), 1)
    select = jnp.concatenate(
        [
            jnp.where((rank[:, i : i + 1] == slots) & (chosen[:, i : i + 1] > 0), 1.0, 0.0)
            for i in range(E_DEV)
        ],
        1,
    ).astype(BF)
    select_common = mm(to_common, select, ((0,), (0,))).astype(BF)
    chosen_rows = mm(select, rows[:, : 2 * lw], ((0,), (0,))).astype(BF)
    all_rows = gather_tp(chosen_rows)

    owner = neuron_expert // E_DEV
    row_i = lax.broadcasted_iota(jnp.int32, (nl, nl), 0)
    col_i = lax.broadcasted_iota(jnp.int32, (nl, nl), 1)
    before = jnp.sum(((owner[:, None] == owner[None, :]) & (col_i < row_i)).astype(jnp.int32), 1)
    target = owner * PEER + before
    packing = (
        target[None, :] == lax.broadcasted_iota(jnp.int32, (n_ep * PEER, nl), 0)
    ).astype(BF)
    label = (neuron_expert % E_DEV * CAPN + neuron_slot + 1).astype(BF)
    common = mm(coefs, to_common, ((1,), (0,))).astype(BF)
    packed = [
        mm(packing, common[i * nl : (i + 1) * nl], ((1,), (0,))).astype(BF) for i in range(3)
    ]
    packed.append(
        mm(packing, jnp.broadcast_to(label[:, None], (nl, 128)), ((1,), (0,))).astype(BF)
    )
    sent = jnp.concatenate(packed, 1).reshape(n_ep, PEER, -1)
    got = lax.all_to_all(sent, "ep", split_axis=0, concat_axis=0, tiled=True)
    got = got.reshape(n_ep * PEER, -1)
    slot_of = got[:, 3 * n_tok].astype(jnp.int32) - 1
    placing = (
        slot_of[None, :] == lax.broadcasted_iota(jnp.int32, (E_DEV * CAPN, n_ep * PEER), 0)
    ).astype(BF)
    grads = []
    for i in range(3):
        placed = mm(placing, got[:, i * n_tok : (i + 1) * n_tok], ((1,), (0,))).astype(BF)
        per_expert = []
        for e in range(E_DEV):
            compact = mm(
                placed[e * CAPN : (e + 1) * CAPN],
                select_common[:, e * TCAP : (e + 1) * TCAP],
                ((1,), (0,)),
            ).astype(BF)
            per_expert.append(compact)
        first = 0 if i < 2 else lw
        grad = jnp.zeros((E_DEV, CAPN, width), BF)
        for dy in range(NY):
            for dc in range(2):
                col = ((y + dy) % NY * 2 + (c + dc) % 2) * lw
                pieces = [
                    mm(
                        per_expert[e],
                        all_rows[dy, dc, e * TCAP : (e + 1) * TCAP, first : first + lw],
                        ((1,), (0,)),
                    ).astype(BF)
                    for e in range(E_DEV)
                ]
                grad = lax.dynamic_update_slice(grad, jnp.stack(pieces, 0), (0, 0, col))
        grads.append(grad)
    return output, d_tokens, d_weight, grads[0], grads[1], grads[2]


def solution(mesh):
    in_specs = (
        P("ep", None),
        P("ep", None),
        P(("tp", "ep"), None),
        P(("tp", "ep"), None),
        P(("tp", "ep"), None),
        P(("tp", "ep")),
        P(("tp", "ep")),
        P("ep", None),
        P("ep", None),
    )
    out_specs = (
        P("ep", "tp"),
        P("ep", "tp"),
        P("ep", None),
        P("ep", "tp", None),
        P("ep", "tp", None),
        P("ep", "tp", None),
    )
    return jax.shard_map(body, mesh=mesh, in_specs=in_specs, out_specs=out_specs, check_vma=False)
```

```python
import jax
import jax.numpy as jnp
from jax import lax
from jax.experimental import pallas as pl
from jax.experimental.pallas import tpu as pltpu
from jax.sharding import PartitionSpec as P


NX = 4
NZ = 8
NY = 4
PEER = 4
CAPN = 64
EXPERTS = 64
E_DEV = 2
TCAP = 128
BF = jnp.bfloat16
F32 = jnp.float32


def move_x(v, s):
    pairs = [(z * NX + x, z * NX + (x + s) % NX) for z in range(NZ) for x in range(NX)]
    return lax.ppermute(v, "ep", pairs)


def move_z(v, s):
    pairs = [(z * NX + x, (z + s) % NZ * NX + x) for z in range(NZ) for x in range(NX)]
    return lax.ppermute(v, "ep", pairs)


def move_y(v, s):
    pairs = [(y * 2 + c, (y + s) % NY * 2 + c) for y in range(NY) for c in range(2)]
    return lax.ppermute(v, "tp", pairs)


def swap_core(v):
    return lax.ppermute(v, "tp", [(i, i ^ 1) for i in range(2 * NY)])


def mm(a, b, dims):
    return lax.dot_general(a, b, (dims, ((), ())), preferred_element_type=F32)


def gather_tokens(block):
    near = jnp.stack(
        [block, move_x(block, -1), move_x(block, -2), move_x(block, 1)],
        0,
    )
    up = [near]
    down = [near]
    for _ in range(3):
        up.append(move_z(up[-1], -1))
        down.append(move_z(down[-1], 1))
    far = jnp.concatenate([move_z(up[3][:2], -1), move_z(down[3][2:], 1)], 0)
    return jnp.stack(up + [far] + down[:0:-1], 1)


def exchange_weights(w_gate, w_up, w_down, y, c):
    two = w_gate.shape[1] // NY
    one = two // 2

    def piece(s):
        start = (y + s) % NY * two
        rows = [lax.dynamic_slice_in_dim(w, start, two, 1) for w in (w_gate, w_up, w_down)]
        return jnp.concatenate(rows, 0)

    before = move_y(piece(1), 1)
    after = move_y(piece(3), -1)
    far = move_y(piece(2), 2)
    got = [piece(0), after, far, before]
    other = jnp.stack([lax.dynamic_slice_in_dim(g, (1 - c) * one, one, 1) for g in got], 0)
    mine = jnp.stack([lax.dynamic_slice_in_dim(g, c * one, one, 1) for g in got], 0)
    return mine, swap_core(other)


def gather_tp(v):
    near = jnp.stack([v] + [move_y(v, -s) for s in range(1, NY)], 0)
    return near, swap_core(near)


def reduce_tp(near, far):
    half = near + swap_core(far.astype(BF)).astype(F32)
    total = half[0]
    for s in range(1, NY):
        total = total + move_y(half[s].astype(BF), s).astype(F32)
    return total


def combine_kernel(order, near, far, w_near, w_far, own, *outs):
    nl = w_near.shape[1] // 3
    lw = w_near.shape[2]
    parts = [(near, w_near, i) for i in range(NY)] + [(far, w_far, i) for i in range(NY)]
    c_h = jnp.concatenate([v[i, 2 * nl : 3 * nl] for v, _, i in parts], 0)
    w_d = jnp.concatenate([w[i, 2 * nl :] for _, w, i in parts], 0)
    c_gu = jnp.concatenate([v[i, : 2 * nl] for v, _, i in parts], 0)
    w_gu = jnp.concatenate([w[i, : 2 * nl] for _, w, i in parts], 0)
    q = sum(v[i, 3 * nl :].astype(F32) for v, _, i in parts)
    q = jnp.concatenate([q, jnp.zeros_like(q)], 0).T.astype(BF)
    tok = own.shape[1]
    out = mm(c_h, w_d, ((0,), (0,))).astype(BF)
    dx = mm(c_gu, w_gu, ((0,), (0,))).astype(BF)
    for k, ref in enumerate((own, *outs)):
        for j in range(NZ):
            rows = slice((k * NZ + j) * tok, (k * NZ + j + 1) * tok)
            ref[order[j], :, :lw] = out[rows]
            ref[order[j], :, lw : 2 * lw] = dx[rows]
            ref[order[j], :, 2 * lw :] = q[rows]


def combine(order, near, far, w_near, w_far):
    n_tok = near.shape[2]
    lw = w_near.shape[2]
    tok = n_tok // (NX * NZ)
    shape = jax.ShapeDtypeStruct((NZ, tok, 2 * lw + 2 * EXPERTS), BF)
    return pl.pallas_call(
        combine_kernel,
        out_shape=(shape,) * NX,
        in_specs=[pl.BlockSpec(memory_space=pltpu.SMEM)]
        + [pl.BlockSpec(memory_space=pltpu.VMEM)] * 4,
        cost_estimate=pl.CostEstimate(
            flops=2 * n_tok * 8 * w_near.shape[1] * lw,
            bytes_accessed=8 * 1024 * 1024,
            transcendentals=0,
        ),
        compiler_params=pltpu.CompilerParams(vmem_limit_bytes=40 * 1024 * 1024),
    )(order, near, far, w_near, w_far)


def reduce_ep(parts):
    moved = [move_x(parts[s], s) for s in range(1, NX)]
    total = parts[0].astype(F32)
    for m in moved:
        total = total + m.astype(F32)
    total = total.astype(BF)
    groups = [[z * NX + x for z in range(NZ)] for x in range(NX)]
    got = lax.all_to_all(
        total, "ep", split_axis=0, concat_axis=0, tiled=True,
        axis_index_groups=groups,
    )
    return jnp.sum(got.astype(F32), 0)


def gather_rows(v):
    near = [v] + [move_y(v, -s) for s in range(1, NY)]
    return near, [swap_core(n) for n in near]


def grads_kernel(cols, got, select, *refs):
    rows = refs[:8]
    outs = refs[8:11]
    buf, sem = refs[11:]
    lw = rows[0].shape[1] // 2
    n_tok = select.shape[0]
    n_out = E_DEV * CAPN
    slot = got[:, 3 * n_tok : 3 * n_tok + n_out].astype(jnp.int32) - 1
    placing = jnp.where(slot == lax.broadcasted_iota(jnp.int32, slot.shape, 1), 1.0, 0.0).astype(BF)
    compact = []
    for i in range(3):
        placed = mm(placing, got[:, i * n_tok : (i + 1) * n_tok], ((0,), (0,))).astype(BF)
        compact.append(
            [
                mm(
                    placed[e * CAPN : (e + 1) * CAPN],
                    select[:, e * TCAP : (e + 1) * TCAP],
                    ((1,), (0,)),
                ).astype(BF)
                for e in range(E_DEV)
            ]
        )
    copies = []
    for j in range(8):
        col = pl.multiple_of(cols[j] * lw, lw)
        for e in range(E_DEV):
            span = slice(e * TCAP, (e + 1) * TCAP)
            both = jnp.concatenate([compact[0][e], compact[1][e]], 0)
            res = mm(both, rows[j][span, :lw], ((1,), (0,))).astype(BF)
            buf[j, 0, e] = res[:CAPN]
            buf[j, 1, e] = res[CAPN:]
            buf[j, 2, e] = mm(compact[2][e], rows[j][span, lw:], ((1,), (0,))).astype(BF)
        for i in range(3):
            copy = pltpu.make_async_copy(
                buf.at[j, i], outs[i].at[:, :, pl.ds(col, lw)], sem.at[j, i]
            )
            copy.start()
            copies.append(copy)
    for copy in copies:
        copy.wait()


def expert_grads(cols, got, select, rows):
    lw = rows[0].shape[1] // 2
    shape = jax.ShapeDtypeStruct((E_DEV, CAPN, 8 * lw), BF)
    vmem = pl.BlockSpec(memory_space=pltpu.VMEM)
    return pl.pallas_call(
        grads_kernel,
        out_shape=(shape, shape, shape),
        in_specs=[pl.BlockSpec(memory_space=pltpu.SMEM)] + [vmem] * 10,
        out_specs=(pl.BlockSpec(memory_space=pl.ANY),) * 3,
        scratch_shapes=[
            pltpu.VMEM((8, 3, E_DEV, CAPN, lw), BF),
            pltpu.SemaphoreType.DMA((8, 3)),
        ],
        cost_estimate=pl.CostEstimate(
            flops=6 * E_DEV * CAPN * TCAP * 8 * lw,
            bytes_accessed=16 * 1024 * 1024,
            transcendentals=0,
        ),
        compiler_params=pltpu.CompilerParams(vmem_limit_bytes=40 * 1024 * 1024),
    )(cols, got, select, *rows)


def body(
    tokens,
    cotangent,
    w_gate,
    w_up,
    w_down,
    neuron_expert,
    neuron_slot,
    choice_expert,
    choice_weight,
):
    t = lax.axis_index("tp")
    ep = lax.axis_index("ep")
    y, c = t // 2, t % 2
    z, x = ep // NX, ep % NX
    n_ep = NX * NZ
    nl, width = w_gate.shape
    tok = tokens.shape[0]
    lw = width // (2 * NY)
    n_tok = n_ep * tok

    experts = lax.broadcasted_iota(jnp.int32, (tok, choice_expert.shape[1], EXPERTS), 2)
    picked = choice_expert[:, :, None] == experts
    dense_w = jnp.sum(jnp.where(picked, choice_weight[:, :, None], 0.0), 1)
    w_hi = dense_w.astype(BF)
    w_lo = (dense_w - w_hi.astype(F32)).astype(BF)
    block = jnp.concatenate(
        [
            lax.dynamic_slice_in_dim(tokens, t * lw, lw, 1),
            lax.dynamic_slice_in_dim(cotangent, t * lw, lw, 1),
            w_hi,
            w_lo,
        ],
        1,
    )
    rows = gather_tokens(block).reshape(n_tok, 2 * lw + 2 * EXPERTS)
    xs = rows[:, :lw]
    cs = rows[:, lw : 2 * lw]
    hi = rows[:, 2 * lw : 2 * lw + EXPERTS]
    lo = rows[:, 2 * lw + EXPERTS :]
    w_near, w_far = exchange_weights(w_gate, w_up, w_down, y, c)

    def partial_sums(w):
        gu = mm(w[:, : 2 * nl].reshape(-1, lw), xs, ((1,), (1,))).reshape(NY, 2 * nl, n_tok)
        d = mm(w[:, 2 * nl :].reshape(-1, lw), cs, ((1,), (1,))).reshape(NY, nl, n_tok)
        return jnp.concatenate([gu, d], 1)

    far_sums = partial_sums(w_far)
    sums = reduce_tp(partial_sums(w_near), far_sums)
    gate, upper, d_raw = sums[:nl], sums[nl : 2 * nl], sums[2 * nl :]

    onehot = (
        neuron_expert[:, None] == lax.broadcasted_iota(jnp.int32, (nl, EXPERTS), 1)
    ).astype(BF)
    scale = mm(onehot, hi, ((1,), (1,))) + mm(onehot, lo, ((1,), (1,)))
    sig = jax.nn.sigmoid(gate)
    silu = gate * sig
    hidden = silu * upper
    dh = d_raw * scale
    coefs = jnp.concatenate(
        [dh * upper * sig * (1.0 + gate * (1.0 - sig)), dh * silu, hidden * scale], 0
    ).astype(BF)
    q_exp = mm(onehot, (hidden * d_raw).astype(BF), ((0,), (0,))).astype(BF)

    near_coefs, far_coefs = gather_tp(jnp.concatenate([coefs, q_exp], 0))
    order = (z + jnp.arange(NZ, dtype=jnp.int32)) % NZ
    parts = combine(order, near_coefs, far_coefs, w_near, w_far)
    final = reduce_ep(parts)
    output = final[:, :lw].astype(BF)
    d_tokens = final[:, lw : 2 * lw].astype(BF)
    q_mine = final[:, 2 * lw : 2 * lw + EXPERTS]
    d_weight = jnp.sum(jnp.where(picked, q_mine[:, None, :], 0.0), 2)

    ri = lax.broadcasted_iota(jnp.int32, (n_tok, n_tok), 0)
    ci = lax.broadcasted_iota(jnp.int32, (n_tok, n_tok), 1)
    per_x = n_tok // NX
    place = (ri // per_x + x) % NX * per_x + (ri // tok % NZ + z) % NZ * tok + ri % tok
    to_common = (place == ci).astype(BF)
    earlier = (ci <= ri).astype(BF)
    own = lax.broadcasted_iota(jnp.int32, (EXPERTS, E_DEV), 0) == (
        ep * E_DEV + lax.broadcasted_iota(jnp.int32, (EXPERTS, E_DEV), 1)
    )
    chosen = (mm(hi, own.astype(BF), ((1,), (0,))) > 0.0).astype(BF)
    rank = mm(earlier, chosen, ((1,), (0,))).astype(jnp.int32) - 1
    slots = lax.broadcasted_iota(jnp.int32, (n_tok, TCAP), 1)
    select = jnp.concatenate(
        [
            jnp.where((rank[:, i : i + 1] == slots) & (chosen[:, i : i + 1] > 0), 1.0, 0.0)
            for i in range(E_DEV)
        ],
        1,
    ).astype(BF)
    select_common = mm(to_common, select, ((0,), (0,))).astype(BF)
    after_coefs = near_coefs[1, 0, 0].astype(F32) * 0.0
    chosen_rows = (mm(select, rows[:, : 2 * lw], ((0,), (0,))) + after_coefs).astype(BF)
    near_rows, far_rows = gather_rows(chosen_rows)

    owner = neuron_expert // E_DEV
    row_i = lax.broadcasted_iota(jnp.int32, (nl, nl), 0)
    col_i = lax.broadcasted_iota(jnp.int32, (nl, nl), 1)
    before = jnp.sum(((owner[:, None] == owner[None, :]) & (col_i < row_i)).astype(jnp.int32), 1)
    target = owner * PEER + before
    packing = (
        target[None, :] == lax.broadcasted_iota(jnp.int32, (n_ep * PEER, nl), 0)
    ).astype(BF)
    label = (neuron_expert % E_DEV * CAPN + neuron_slot + 1).astype(BF)
    common = mm(coefs, to_common, ((1,), (0,))).astype(BF)
    packed = [mm(packing, common[i * nl : (i + 1) * nl], ((1,), (0,))).astype(BF) for i in range(3)]
    tag = jnp.broadcast_to(label[:, None], (nl, 128))
    packed.append(mm(packing, tag, ((1,), (0,))).astype(BF))
    sent = jnp.concatenate(packed, 1).reshape(n_ep, PEER, -1)
    got = lax.all_to_all(sent, "ep", split_axis=0, concat_axis=0, tiled=True)
    got = got.reshape(n_ep * PEER, -1)
    turns = jnp.arange(8, dtype=jnp.int32)
    cols = (y + turns % NY) % NY * 2 + (c + turns // NY) % 2
    grads = expert_grads(cols, got, select_common, near_rows + far_rows)
    return output, d_tokens, d_weight, grads[0], grads[1], grads[2]


def solution(mesh):
    in_specs = (
        P("ep", None),
        P("ep", None),
        P(("tp", "ep"), None),
        P(("tp", "ep"), None),
        P(("tp", "ep"), None),
        P(("tp", "ep")),
        P(("tp", "ep")),
        P("ep", None),
        P("ep", None),
    )
    out_specs = (
        P("ep", "tp"),
        P("ep", "tp"),
        P("ep", None),
        P("ep", "tp", None),
        P("ep", "tp", None),
        P("ep", "tp", None),
    )

    return jax.shard_map(body, mesh=mesh, in_specs=in_specs, out_specs=out_specs, check_vma=False)
```

```python
import jax
import jax.numpy as jnp
from jax import lax
from jax.experimental import pallas as pl
from jax.experimental.pallas import tpu as pltpu
from jax.sharding import PartitionSpec as P


NX = 4
NZ = 8
NY = 4
PEER = 4
CAPN = 64
EXPERTS = 64
E_DEV = 2
TCAP = 128
BF = jnp.bfloat16
F32 = jnp.float32


def move_x(v, s):
    pairs = [(z * NX + x, z * NX + (x + s) % NX) for z in range(NZ) for x in range(NX)]
    return lax.ppermute(v, "ep", pairs)


def move_z(v, s):
    pairs = [(z * NX + x, (z + s) % NZ * NX + x) for z in range(NZ) for x in range(NX)]
    return lax.ppermute(v, "ep", pairs)


def move_y(v, s):
    pairs = [(y * 2 + c, (y + s) % NY * 2 + c) for y in range(NY) for c in range(2)]
    return lax.ppermute(v, "tp", pairs)


def swap_core(v):
    return lax.ppermute(v, "tp", [(i, i ^ 1) for i in range(2 * NY)])


def mm(a, b, dims):
    return lax.dot_general(a, b, (dims, ((), ())), preferred_element_type=F32)


def gather_tokens(block):
    near = jnp.stack(
        [block, move_x(block, -1), move_x(block, -2), move_x(block, 1)],
        0,
    )
    up = [near]
    down = [near]
    for _ in range(3):
        up.append(move_z(up[-1], -1))
        down.append(move_z(down[-1], 1))
    far = jnp.concatenate([move_z(up[3][:2], -1), move_z(down[3][2:], 1)], 0)
    return jnp.stack(up + [far] + down[:0:-1], 1)


def exchange_weights(w_gate, w_up, w_down, y, c):
    two = w_gate.shape[1] // NY
    one = two // 2

    def piece(s):
        start = (y + s) % NY * two
        rows = [lax.dynamic_slice_in_dim(w, start, two, 1) for w in (w_gate, w_up, w_down)]
        return jnp.concatenate(rows, 0)

    before = move_y(piece(1), 1)
    after = move_y(piece(3), -1)
    far = move_y(piece(2), 2)
    got = [piece(0), after, far, before]
    other = jnp.stack([lax.dynamic_slice_in_dim(g, (1 - c) * one, one, 1) for g in got], 0)
    mine = jnp.stack([lax.dynamic_slice_in_dim(g, c * one, one, 1) for g in got], 0)
    return mine, swap_core(other)


def gather_tp(v):
    near = jnp.stack([v] + [move_y(v, -s) for s in range(1, NY)], 0)
    return near, swap_core(near)


def reduce_tp(near, far):
    half = near + swap_core(far.astype(BF)).astype(F32)
    total = half[0]
    for s in range(1, NY):
        total = total + move_y(half[s].astype(BF), s).astype(F32)
    return total


def combine_kernel(order, near, far, w_near, w_far, own, *refs):
    outs = refs[:-1]
    held = refs[-1]
    n_blocks = held.shape[0]
    nl = w_near.shape[1] // 3
    lw = w_near.shape[2]
    parts = [(near, w_near, i) for i in range(NY)] + [(far, w_far, i) for i in range(NY)]
    c_h = jnp.concatenate([v[i, 2 * nl : 3 * nl] for v, _, i in parts], 0)
    w_d = jnp.concatenate([w[i, 2 * nl :] for _, w, i in parts], 0)
    c_gu = jnp.concatenate([v[i, : 2 * nl] for v, _, i in parts], 0)
    w_gu = jnp.concatenate([w[i, : 2 * nl] for _, w, i in parts], 0)
    q = sum(v[i, 3 * nl :].astype(F32) for v, _, i in parts)
    q = jnp.concatenate([q, jnp.zeros_like(q)], 0).T.astype(BF)
    tok = own.shape[1]
    whole = (n_blocks, tok)
    held[:, :, :lw] = mm(c_h, w_d, ((0,), (0,))).astype(BF).reshape(*whole, lw)
    held[:, :, lw : 2 * lw] = mm(c_gu, w_gu, ((0,), (0,))).astype(BF).reshape(*whole, lw)
    held[:, :, 2 * lw :] = q.reshape(*whole, 2 * EXPERTS)

    def store(j, carry):
        for k, ref in enumerate((own, *outs)):
            ref[order[j]] = held[k * NZ + j]
        return carry

    lax.fori_loop(0, NZ, store, 0)


def combine(order, near, far, w_near, w_far):
    n_tok = near.shape[2]
    lw = w_near.shape[2]
    tok = n_tok // (NX * NZ)
    shape = jax.ShapeDtypeStruct((NZ, tok, 2 * lw + 2 * EXPERTS), BF)
    return pl.pallas_call(
        combine_kernel,
        out_shape=(shape,) * NX,
        scratch_shapes=[pltpu.VMEM((NX * NZ, *shape.shape[1:]), BF)],
        in_specs=[pl.BlockSpec(memory_space=pltpu.SMEM)]
        + [pl.BlockSpec(memory_space=pltpu.VMEM)] * 4,
        cost_estimate=pl.CostEstimate(
            flops=2 * n_tok * 8 * w_near.shape[1] * lw,
            bytes_accessed=8 * 1024 * 1024,
            transcendentals=0,
        ),
        compiler_params=pltpu.CompilerParams(vmem_limit_bytes=40 * 1024 * 1024),
    )(order, near, far, w_near, w_far)


def reduce_ep(parts):
    moved = [move_x(parts[s], s) for s in range(1, NX)]
    total = parts[0].astype(F32)
    for m in moved:
        total = total + m.astype(F32)
    total = total.astype(BF)
    groups = [[z * NX + x for z in range(NZ)] for x in range(NX)]
    got = lax.all_to_all(
        total, "ep", split_axis=0, concat_axis=0, tiled=True,
        axis_index_groups=groups,
    )
    return jnp.sum(got.astype(F32), 0)


def gather_rows(v):
    mid = v.shape[0] // 2
    after = move_y(v, -1)
    before = move_y(v, 1)
    via_after = move_y(after[:mid], -1)
    via_before = move_y(before[mid:], 1)
    near = [v, after, via_after, via_before, before]
    return near, [swap_core(n) for n in near]


def grads_kernel(cols, got, select, *refs):
    rows = refs[:10]
    outs = refs[10:13]
    held, coef, buf, in_sem, out_sem = refs[13:]
    mid = held.shape[1] // 2
    for h in range(2):
        part = rows[5 * h : 5 * h + 5]
        j = NY * h
        pltpu.make_async_copy(part[0], held.at[j], in_sem.at[j]).start()
        pltpu.make_async_copy(part[1], held.at[j + 1], in_sem.at[j + 1]).start()
        pltpu.make_async_copy(part[2], held.at[j + 2, :mid], in_sem.at[j + 2]).start()
        pltpu.make_async_copy(part[3], held.at[j + 2, mid:], in_sem.at[j + 2]).start()
        pltpu.make_async_copy(part[4], held.at[j + 3], in_sem.at[j + 3]).start()
    lw = held.shape[2] // 2
    n_tok = select.shape[0]
    n_out = E_DEV * CAPN
    slot = got[:, 3 * n_tok : 3 * n_tok + n_out].astype(jnp.int32) - 1
    placing = jnp.where(slot == lax.broadcasted_iota(jnp.int32, slot.shape, 1), 1.0, 0.0).astype(BF)
    placed = mm(placing, got[:, : 3 * n_tok], ((0,), (0,))).astype(BF)
    for e in range(E_DEV):
        mine = placed[e * CAPN : (e + 1) * CAPN]
        stack = jnp.concatenate([mine[:, i * n_tok : (i + 1) * n_tok] for i in range(3)], 0)
        coef[e] = mm(stack, select[:, e * TCAP : (e + 1) * TCAP], ((1,), (0,))).astype(BF)

    def out_copy(j, i, col):
        return pltpu.make_async_copy(
            buf.at[j, i], outs[i].at[:, :, pl.ds(col, lw)], out_sem.at[j, i]
        )

    def step(j, carry):
        pltpu.make_async_copy(rows[0], held.at[j], in_sem.at[j]).wait()
        col = pl.multiple_of(cols[j] * lw, lw)
        for e in range(E_DEV):
            span = slice(e * TCAP, (e + 1) * TCAP)
            res = mm(coef[e, : 2 * CAPN], held[j, span, :lw], ((1,), (0,))).astype(BF)
            buf[j, 0, e] = res[:CAPN]
            buf[j, 1, e] = res[CAPN:]
            buf[j, 2, e] = mm(coef[e, 2 * CAPN :], held[j, span, lw:], ((1,), (0,))).astype(BF)
        for i in range(3):
            out_copy(j, i, col).start()
        return carry

    def drain(j, carry):
        for i in range(3):
            out_copy(j, i, 0).wait()
        return carry

    lax.fori_loop(0, 8, step, 0)
    lax.fori_loop(0, 8, drain, 0)


def expert_grads(cols, got, select, rows):
    lw = rows[0].shape[1] // 2
    shape = jax.ShapeDtypeStruct((E_DEV, CAPN, 8 * lw), BF)
    vmem = pl.BlockSpec(memory_space=pltpu.VMEM)
    return pl.pallas_call(
        grads_kernel,
        out_shape=(shape, shape, shape),
        in_specs=[pl.BlockSpec(memory_space=pltpu.SMEM), vmem, vmem]
        + [pl.BlockSpec(memory_space=pl.ANY)] * 10,
        out_specs=(pl.BlockSpec(memory_space=pl.ANY),) * 3,
        scratch_shapes=[
            pltpu.VMEM((8, *rows[0].shape), BF),
            pltpu.VMEM((E_DEV, 3 * CAPN, TCAP), BF),
            pltpu.VMEM((8, 3, E_DEV, CAPN, lw), BF),
            pltpu.SemaphoreType.DMA((8,)),
            pltpu.SemaphoreType.DMA((8, 3)),
        ],
        cost_estimate=pl.CostEstimate(
            flops=6 * E_DEV * CAPN * TCAP * 8 * lw,
            bytes_accessed=16 * 1024 * 1024,
            transcendentals=0,
        ),
        compiler_params=pltpu.CompilerParams(vmem_limit_bytes=40 * 1024 * 1024),
    )(cols, got, select, *rows)


def body(
    tokens,
    cotangent,
    w_gate,
    w_up,
    w_down,
    neuron_expert,
    neuron_slot,
    choice_expert,
    choice_weight,
):
    t = lax.axis_index("tp")
    ep = lax.axis_index("ep")
    y, c = t // 2, t % 2
    z, x = ep // NX, ep % NX
    n_ep = NX * NZ
    nl, width = w_gate.shape
    tok = tokens.shape[0]
    lw = width // (2 * NY)
    n_tok = n_ep * tok

    experts = lax.broadcasted_iota(jnp.int32, (tok, choice_expert.shape[1], EXPERTS), 2)
    picked = choice_expert[:, :, None] == experts
    dense_w = jnp.sum(jnp.where(picked, choice_weight[:, :, None], 0.0), 1)
    w_hi = dense_w.astype(BF)
    w_lo = (dense_w - w_hi.astype(F32)).astype(BF)
    block = jnp.concatenate(
        [
            lax.dynamic_slice_in_dim(tokens, t * lw, lw, 1),
            lax.dynamic_slice_in_dim(cotangent, t * lw, lw, 1),
            w_hi,
            w_lo,
        ],
        1,
    )
    rows = gather_tokens(block).reshape(n_tok, 2 * lw + 2 * EXPERTS)
    xs = rows[:, :lw]
    cs = rows[:, lw : 2 * lw]
    hi = rows[:, 2 * lw : 2 * lw + EXPERTS]
    hi_lo = rows[:, 2 * lw :]
    w_near, w_far = exchange_weights(w_gate, w_up, w_down, y, c)

    def partial_sums(w):
        gu = mm(w[:, : 2 * nl].reshape(-1, lw), xs, ((1,), (1,))).reshape(NY, 2 * nl, n_tok)
        d = mm(w[:, 2 * nl :].reshape(-1, lw), cs, ((1,), (1,))).reshape(NY, nl, n_tok)
        return jnp.concatenate([gu, d], 1)

    far_sums = partial_sums(w_far)
    sums = reduce_tp(partial_sums(w_near), far_sums)
    gate, upper, d_raw = sums[:nl], sums[nl : 2 * nl], sums[2 * nl :]

    onehot = (
        neuron_expert[:, None] == lax.broadcasted_iota(jnp.int32, (nl, EXPERTS), 1)
    ).astype(BF)
    scale = mm(jnp.concatenate([onehot, onehot], 1), hi_lo, ((1,), (1,)))
    sig = jax.nn.sigmoid(gate)
    silu = gate * sig
    hidden = silu * upper
    dh = d_raw * scale
    coefs = jnp.concatenate(
        [dh * upper * sig * (1.0 + gate * (1.0 - sig)), dh * silu, hidden * scale], 0
    ).astype(BF)
    q_exp = mm(onehot, (hidden * d_raw).astype(BF), ((0,), (0,))).astype(BF)

    near_coefs, far_coefs = gather_tp(jnp.concatenate([coefs, q_exp], 0))
    order = (z + jnp.arange(NZ, dtype=jnp.int32)) % NZ
    parts = combine(order, near_coefs, far_coefs, w_near, w_far)
    final = reduce_ep(parts)
    output = final[:, :lw].astype(BF)
    d_tokens = final[:, lw : 2 * lw].astype(BF)
    q_mine = final[:, 2 * lw : 2 * lw + EXPERTS]
    d_weight = jnp.sum(jnp.where(picked, q_mine[:, None, :], 0.0), 2)

    ri = lax.broadcasted_iota(jnp.int32, (n_tok, n_tok), 0)
    ci = lax.broadcasted_iota(jnp.int32, (n_tok, n_tok), 1)
    per_x = n_tok // NX
    place = (ri // per_x + x) % NX * per_x + (ri // tok % NZ + z) % NZ * tok + ri % tok
    to_common = (place == ci).astype(BF)
    earlier = (ci <= ri).astype(BF)
    own = lax.broadcasted_iota(jnp.int32, (EXPERTS, E_DEV), 0) == (
        ep * E_DEV + lax.broadcasted_iota(jnp.int32, (EXPERTS, E_DEV), 1)
    )
    chosen = (mm(hi, own.astype(BF), ((1,), (0,))) > 0.0).astype(BF)
    rank = mm(earlier, chosen, ((1,), (0,))).astype(jnp.int32) - 1
    slots = lax.broadcasted_iota(jnp.int32, (n_tok, TCAP), 1)
    select = jnp.concatenate(
        [
            jnp.where((rank[:, i : i + 1] == slots) & (chosen[:, i : i + 1] > 0), 1.0, 0.0)
            for i in range(E_DEV)
        ],
        1,
    ).astype(BF)
    select_common = mm(to_common, select, ((0,), (0,))).astype(BF)
    chosen_rows = mm(select, rows[:, : 2 * lw], ((0,), (0,))).astype(BF)
    near_rows, far_rows = gather_rows(chosen_rows)

    owner = neuron_expert // E_DEV
    row_i = lax.broadcasted_iota(jnp.int32, (nl, nl), 0)
    col_i = lax.broadcasted_iota(jnp.int32, (nl, nl), 1)
    before = jnp.sum(((owner[:, None] == owner[None, :]) & (col_i < row_i)).astype(jnp.int32), 1)
    target = owner * PEER + before
    packing = (target[None, :] == lax.broadcasted_iota(jnp.int32, (n_ep * PEER, nl), 0)).astype(BF)
    label = (neuron_expert % E_DEV * CAPN + neuron_slot + 1).astype(BF)
    common = mm(coefs, to_common, ((1,), (0,))).astype(BF)
    tag = jnp.broadcast_to(label[:, None], (nl, 128))
    wide = [common[i * nl : (i + 1) * nl] for i in range(3)] + [tag]
    sent = mm(packing, jnp.concatenate(wide, 1), ((1,), (0,))).astype(BF)
    sent = sent.reshape(n_ep, PEER, -1)
    got = lax.all_to_all(sent, "ep", split_axis=0, concat_axis=0, tiled=True)
    got = got.reshape(n_ep * PEER, -1)
    turns = jnp.arange(8, dtype=jnp.int32)
    cols = (y + turns % NY) % NY * 2 + (c + turns // NY) % 2
    grads = expert_grads(cols, got, select_common, near_rows + far_rows)
    return output, d_tokens, d_weight, grads[0], grads[1], grads[2]


def solution(mesh):
    in_specs = (
        P("ep", None),
        P("ep", None),
        P(("tp", "ep"), None),
        P(("tp", "ep"), None),
        P(("tp", "ep"), None),
        P(("tp", "ep")),
        P(("tp", "ep")),
        P("ep", None),
        P("ep", None),
    )
    out_specs = (
        P("ep", "tp"),
        P("ep", "tp"),
        P("ep", None),
        P("ep", "tp", None),
        P("ep", "tp", None),
        P("ep", "tp", None),
    )

    return jax.shard_map(body, mesh=mesh, in_specs=in_specs, out_specs=out_specs, check_vma=False)
```

```python
import jax
import jax.numpy as jnp
from jax import lax
from jax.experimental import pallas as pl
from jax.experimental.pallas import tpu as pltpu
from jax.sharding import PartitionSpec as P


NX = 4
NZ = 8
NY = 4
PEER = 4
CAPN = 64
EXPERTS = 64
E_DEV = 2
TCAP = 128
BF = jnp.bfloat16
F32 = jnp.float32


def move_x(v, s):
    pairs = [(z * NX + x, z * NX + (x + s) % NX) for z in range(NZ) for x in range(NX)]
    return lax.ppermute(v, "ep", pairs)


def move_z(v, s):
    pairs = [(z * NX + x, (z + s) % NZ * NX + x) for z in range(NZ) for x in range(NX)]
    return lax.ppermute(v, "ep", pairs)


def move_y(v, s):
    pairs = [(y * 2 + c, (y + s) % NY * 2 + c) for y in range(NY) for c in range(2)]
    return lax.ppermute(v, "tp", pairs)


def swap_core(v):
    return lax.ppermute(v, "tp", [(i, i ^ 1) for i in range(2 * NY)])


def mm(a, b, dims):
    return lax.dot_general(a, b, (dims, ((), ())), preferred_element_type=F32)


def gather_tokens(block):
    near = jnp.stack(
        [block, move_x(block, -1), move_x(block, -2), move_x(block, 1)],
        0,
    )
    up = [near]
    down = [near]
    for _ in range(3):
        up.append(move_z(up[-1], -1))
        down.append(move_z(down[-1], 1))
    far = jnp.concatenate([move_z(up[3][:2], -1), move_z(down[3][2:], 1)], 0)
    return jnp.stack(up + [far] + down[:0:-1], 1)


def exchange_weights(w_gate, w_up, w_down, y, c):
    two = w_gate.shape[1] // NY
    one = two // 2

    def piece(s):
        start = (y + s) % NY * two
        rows = [lax.dynamic_slice_in_dim(w, start, two, 1) for w in (w_gate, w_up, w_down)]
        return jnp.concatenate(rows, 0)

    before = move_y(piece(1), 1)
    after = move_y(piece(3), -1)
    far = move_y(piece(2), 2)
    got = [piece(0), after, far, before]
    other = jnp.stack([lax.dynamic_slice_in_dim(g, (1 - c) * one, one, 1) for g in got], 0)
    mine = jnp.stack([lax.dynamic_slice_in_dim(g, c * one, one, 1) for g in got], 0)
    return mine, swap_core(other)


def gather_tp(v):
    near = jnp.stack([v] + [move_y(v, -s) for s in range(1, NY)], 0)
    return near, swap_core(near)


def reduce_tp(near, far):
    half = near + swap_core(far.astype(BF)).astype(F32)
    total = half[0]
    for s in range(1, NY):
        total = total + move_y(half[s].astype(BF), s).astype(F32)
    return total


def combine_kernel(order, near, far, w_near, w_far, own, *refs):
    outs = refs[:-1]
    held = refs[-1]
    n_blocks = held.shape[0]
    nl = w_near.shape[1] // 3
    lw = w_near.shape[2]
    parts = [(near, w_near, i) for i in range(NY)] + [(far, w_far, i) for i in range(NY)]
    c_h = jnp.concatenate([v[i, 2 * nl : 3 * nl] for v, _, i in parts], 0)
    w_d = jnp.concatenate([w[i, 2 * nl :] for _, w, i in parts], 0)
    c_gu = jnp.concatenate([v[i, : 2 * nl] for v, _, i in parts], 0)
    w_gu = jnp.concatenate([w[i, : 2 * nl] for _, w, i in parts], 0)
    q = sum(v[i, 3 * nl :].astype(F32) for v, _, i in parts)
    q = jnp.concatenate([q, jnp.zeros_like(q)], 0).T.astype(BF)
    halves = (own, *outs)
    tok = own.shape[1]
    whole = (n_blocks, tok)
    held[:, :, :lw] = mm(c_h, w_d, ((0,), (0,))).astype(BF).reshape(*whole, lw)
    held[:, :, lw : 2 * lw] = mm(c_gu, w_gu, ((0,), (0,))).astype(BF).reshape(*whole, lw)
    held[:, :, 2 * lw :] = q.reshape(*whole, 2 * EXPERTS)

    def store(j, carry):
        spot = order[j] % (NZ // 2)

        @pl.when(order[j] < NZ // 2)
        def _():
            for k in range(NX):
                halves[2 * k][spot] = held[k * NZ + j]

        @pl.when(order[j] >= NZ // 2)
        def _():
            for k in range(NX):
                halves[2 * k + 1][spot] = held[k * NZ + j]

        return carry

    lax.fori_loop(0, NZ, store, 0)


def combine(order, near, far, w_near, w_far):
    n_tok = near.shape[2]
    lw = w_near.shape[2]
    tok = n_tok // (NX * NZ)
    shape = jax.ShapeDtypeStruct((NZ // 2, tok, 2 * lw + 2 * EXPERTS), BF)
    return pl.pallas_call(
        combine_kernel,
        out_shape=(shape,) * (2 * NX),
        scratch_shapes=[pltpu.VMEM((NX * NZ, *shape.shape[1:]), BF)],
        in_specs=[pl.BlockSpec(memory_space=pltpu.SMEM)]
        + [pl.BlockSpec(memory_space=pltpu.VMEM)] * 4,
        cost_estimate=pl.CostEstimate(
            flops=2 * n_tok * 8 * w_near.shape[1] * lw,
            bytes_accessed=8 * 1024 * 1024,
            transcendentals=0,
        ),
        compiler_params=pltpu.CompilerParams(vmem_limit_bytes=40 * 1024 * 1024),
    )(order, near, far, w_near, w_far)


def reduce_ep(parts):
    via_up = move_x(parts[4], 1)
    via_down = move_x(parts[5], -1)
    near_up = move_x(parts[3], 1)
    near_down = move_x(parts[6], -1)
    acc_up = (parts[2].astype(F32) + via_up.astype(F32)).astype(BF)
    acc_down = (parts[7].astype(F32) + via_down.astype(F32)).astype(BF)
    sum_up = move_x(acc_up, 1)
    sum_down = move_x(acc_down, -1)
    groups = [[z * NX + x for z in range(NZ)] for x in range(NX)]
    low = parts[0].astype(F32) + near_down.astype(F32) + sum_up.astype(F32)
    high = parts[1].astype(F32) + near_up.astype(F32) + sum_down.astype(F32)
    total = jnp.concatenate([low.astype(BF), high.astype(BF)], 0)
    got = lax.all_to_all(
        total, "ep", split_axis=0, concat_axis=0, tiled=True, axis_index_groups=groups
    )
    return jnp.sum(got.astype(F32), 0)


def gather_rows(v):
    mid = v.shape[0] // 2
    after = move_y(v, -1)
    before = move_y(v, 1)
    via_after = move_y(after[:mid], -1)
    via_before = move_y(before[mid:], 1)
    near = [v, after, via_after, via_before, before]
    return near, [swap_core(n) for n in near]


def grads_kernel(cols, got, select, *refs):
    rows = refs[:10]
    outs = refs[10:13]
    held, coef, buf, in_sem, out_sem = refs[13:]
    mid = held.shape[1] // 2
    for h in range(2):
        part = rows[5 * h : 5 * h + 5]
        j = NY * h
        pltpu.make_async_copy(part[0], held.at[j], in_sem.at[j]).start()
        pltpu.make_async_copy(part[1], held.at[j + 1], in_sem.at[j + 1]).start()
        pltpu.make_async_copy(part[2], held.at[j + 2, :mid], in_sem.at[j + 2]).start()
        pltpu.make_async_copy(part[3], held.at[j + 2, mid:], in_sem.at[j + 2]).start()
        pltpu.make_async_copy(part[4], held.at[j + 3], in_sem.at[j + 3]).start()
    lw = held.shape[2] // 2
    n_tok = select.shape[0]
    n_out = E_DEV * CAPN
    slot = got[:, 3 * n_tok : 3 * n_tok + n_out].astype(jnp.int32) - 1
    placing = jnp.where(slot == lax.broadcasted_iota(jnp.int32, slot.shape, 1), 1.0, 0.0).astype(BF)
    placed = mm(placing, got[:, : 3 * n_tok], ((0,), (0,))).astype(BF)
    for e in range(E_DEV):
        mine = placed[e * CAPN : (e + 1) * CAPN]
        stack = jnp.concatenate([mine[:, i * n_tok : (i + 1) * n_tok] for i in range(3)], 0)
        coef[e] = mm(stack, select[:, e * TCAP : (e + 1) * TCAP], ((1,), (0,))).astype(BF)

    def out_copy(j, i, col):
        return pltpu.make_async_copy(
            buf.at[j, i], outs[i].at[:, :, pl.ds(col, lw)], out_sem.at[j, i]
        )

    def step(j, carry):
        pltpu.make_async_copy(rows[0], held.at[j], in_sem.at[j]).wait()
        col = pl.multiple_of(cols[j] * lw, lw)
        for e in range(E_DEV):
            span = slice(e * TCAP, (e + 1) * TCAP)
            res = mm(coef[e, : 2 * CAPN], held[j, span, :lw], ((1,), (0,))).astype(BF)
            buf[j, 0, e] = res[:CAPN]
            buf[j, 1, e] = res[CAPN:]
            buf[j, 2, e] = mm(coef[e, 2 * CAPN :], held[j, span, lw:], ((1,), (0,))).astype(BF)
        for i in range(3):
            out_copy(j, i, col).start()
        return carry

    def drain(j, carry):
        for i in range(3):
            out_copy(j, i, 0).wait()
        return carry

    lax.fori_loop(0, 8, step, 0)
    lax.fori_loop(0, 8, drain, 0)


def expert_grads(cols, got, select, rows):
    lw = rows[0].shape[1] // 2
    shape = jax.ShapeDtypeStruct((E_DEV, CAPN, 8 * lw), BF)
    vmem = pl.BlockSpec(memory_space=pltpu.VMEM)
    return pl.pallas_call(
        grads_kernel,
        out_shape=(shape, shape, shape),
        in_specs=[pl.BlockSpec(memory_space=pltpu.SMEM), vmem, vmem]
        + [pl.BlockSpec(memory_space=pl.ANY)] * 10,
        out_specs=(pl.BlockSpec(memory_space=pl.ANY),) * 3,
        scratch_shapes=[
            pltpu.VMEM((8, *rows[0].shape), BF),
            pltpu.VMEM((E_DEV, 3 * CAPN, TCAP), BF),
            pltpu.VMEM((8, 3, E_DEV, CAPN, lw), BF),
            pltpu.SemaphoreType.DMA((8,)),
            pltpu.SemaphoreType.DMA((8, 3)),
        ],
        cost_estimate=pl.CostEstimate(
            flops=6 * E_DEV * CAPN * TCAP * 8 * lw,
            bytes_accessed=16 * 1024 * 1024,
            transcendentals=0,
        ),
        compiler_params=pltpu.CompilerParams(vmem_limit_bytes=40 * 1024 * 1024),
    )(cols, got, select, *rows)


def body(
    tokens,
    cotangent,
    w_gate,
    w_up,
    w_down,
    neuron_expert,
    neuron_slot,
    choice_expert,
    choice_weight,
):
    t = lax.axis_index("tp")
    ep = lax.axis_index("ep")
    y, c = t // 2, t % 2
    z, x = ep // NX, ep % NX
    n_ep = NX * NZ
    nl, width = w_gate.shape
    tok = tokens.shape[0]
    lw = width // (2 * NY)
    n_tok = n_ep * tok

    experts = lax.broadcasted_iota(jnp.int32, (tok, choice_expert.shape[1], EXPERTS), 2)
    picked = choice_expert[:, :, None] == experts
    dense_w = jnp.sum(jnp.where(picked, choice_weight[:, :, None], 0.0), 1)
    w_hi = dense_w.astype(BF)
    w_lo = (dense_w - w_hi.astype(F32)).astype(BF)
    block = jnp.concatenate(
        [
            lax.dynamic_slice_in_dim(tokens, t * lw, lw, 1),
            lax.dynamic_slice_in_dim(cotangent, t * lw, lw, 1),
            w_hi,
            w_lo,
        ],
        1,
    )
    rows = gather_tokens(block).reshape(n_tok, 2 * lw + 2 * EXPERTS)
    xs = rows[:, :lw]
    cs = rows[:, lw : 2 * lw]
    hi = rows[:, 2 * lw : 2 * lw + EXPERTS]
    hi_lo = rows[:, 2 * lw :]
    w_near, w_far = exchange_weights(w_gate, w_up, w_down, y, c)

    def partial_sums(w):
        gu = mm(w[:, : 2 * nl].reshape(-1, lw), xs, ((1,), (1,))).reshape(NY, 2 * nl, n_tok)
        d = mm(w[:, 2 * nl :].reshape(-1, lw), cs, ((1,), (1,))).reshape(NY, nl, n_tok)
        return jnp.concatenate([gu, d], 1)

    far_sums = partial_sums(w_far)
    sums = reduce_tp(partial_sums(w_near), far_sums)
    gate, upper, d_raw = sums[:nl], sums[nl : 2 * nl], sums[2 * nl :]

    onehot = (
        neuron_expert[:, None] == lax.broadcasted_iota(jnp.int32, (nl, EXPERTS), 1)
    ).astype(BF)
    scale = mm(jnp.concatenate([onehot, onehot], 1), hi_lo, ((1,), (1,)))
    sig = jax.nn.sigmoid(gate)
    silu = gate * sig
    hidden = silu * upper
    dh = d_raw * scale
    coefs = jnp.concatenate(
        [dh * upper * sig * (1.0 + gate * (1.0 - sig)), dh * silu, hidden * scale], 0
    ).astype(BF)
    q_exp = mm(onehot, (hidden * d_raw).astype(BF), ((0,), (0,))).astype(BF)

    near_coefs, far_coefs = gather_tp(jnp.concatenate([coefs, q_exp], 0))
    order = (z + jnp.arange(NZ, dtype=jnp.int32)) % NZ
    parts = combine(order, near_coefs, far_coefs, w_near, w_far)
    final = reduce_ep(parts)
    output = final[:, :lw].astype(BF)
    d_tokens = final[:, lw : 2 * lw].astype(BF)
    q_mine = final[:, 2 * lw : 2 * lw + EXPERTS]
    d_weight = jnp.sum(jnp.where(picked, q_mine[:, None, :], 0.0), 2)

    ri = lax.broadcasted_iota(jnp.int32, (n_tok, n_tok), 0)
    ci = lax.broadcasted_iota(jnp.int32, (n_tok, n_tok), 1)
    per_x = n_tok // NX
    place = (ri // per_x + x) % NX * per_x + (ri // tok % NZ + z) % NZ * tok + ri % tok
    to_common = (place == ci).astype(BF)
    earlier = (ci <= ri).astype(BF)
    own = lax.broadcasted_iota(jnp.int32, (EXPERTS, E_DEV), 0) == (
        ep * E_DEV + lax.broadcasted_iota(jnp.int32, (EXPERTS, E_DEV), 1)
    )
    chosen = (mm(hi, own.astype(BF), ((1,), (0,))) > 0.0).astype(BF)
    rank = mm(earlier, chosen, ((1,), (0,))).astype(jnp.int32) - 1
    slots = lax.broadcasted_iota(jnp.int32, (n_tok, TCAP), 1)
    select = jnp.concatenate(
        [
            jnp.where((rank[:, i : i + 1] == slots) & (chosen[:, i : i + 1] > 0), 1.0, 0.0)
            for i in range(E_DEV)
        ],
        1,
    ).astype(BF)
    select_common = mm(to_common, select, ((0,), (0,))).astype(BF)
    chosen_rows = mm(select, rows[:, : 2 * lw], ((0,), (0,))).astype(BF)
    near_rows, far_rows = gather_rows(chosen_rows)

    owner = neuron_expert // E_DEV
    row_i = lax.broadcasted_iota(jnp.int32, (nl, nl), 0)
    col_i = lax.broadcasted_iota(jnp.int32, (nl, nl), 1)
    before = jnp.sum(((owner[:, None] == owner[None, :]) & (col_i < row_i)).astype(jnp.int32), 1)
    target = owner * PEER + before
    packing = (target[None, :] == lax.broadcasted_iota(jnp.int32, (n_ep * PEER, nl), 0)).astype(BF)
    label = (neuron_expert % E_DEV * CAPN + neuron_slot + 1).astype(BF)
    common = mm(coefs, to_common, ((1,), (0,))).astype(BF)
    tag = jnp.broadcast_to(label[:, None], (nl, 128))
    wide = [common[i * nl : (i + 1) * nl] for i in range(3)] + [tag]
    sent = mm(packing, jnp.concatenate(wide, 1), ((1,), (0,))).astype(BF)
    sent = sent.reshape(n_ep, PEER, -1)
    got = lax.all_to_all(sent, "ep", split_axis=0, concat_axis=0, tiled=True)
    got = got.reshape(n_ep * PEER, -1)
    turns = jnp.arange(8, dtype=jnp.int32)
    cols = (y + turns % NY) % NY * 2 + (c + turns // NY) % 2
    grads = expert_grads(cols, got, select_common, near_rows + far_rows)
    return output, d_tokens, d_weight, grads[0], grads[1], grads[2]


def solution(mesh):
    in_specs = (
        P("ep", None),
        P("ep", None),
        P(("tp", "ep"), None),
        P(("tp", "ep"), None),
        P(("tp", "ep"), None),
        P(("tp", "ep")),
        P(("tp", "ep")),
        P("ep", None),
        P("ep", None),
    )
    out_specs = (
        P("ep", "tp"),
        P("ep", "tp"),
        P("ep", None),
        P("ep", "tp", None),
        P("ep", "tp", None),
        P("ep", "tp", None),
    )

    return jax.shard_map(body, mesh=mesh, in_specs=in_specs, out_specs=out_specs, check_vma=False)
```
